32 devices in a mesh: energy: 8 (over z, x), region: 4 (over y, core).
Axes of the slice: x: 2, y: 2, z: 4, core: 2. Of those that a mesh axis runs over, the one named last changes fastest.
Arguments:
- onsite: float32 [4, 2, 128, 128], P('region'), may hold values from -0.5 to 0.5
- coupling: float32 [4, 2, 128, 128], P('region'), may hold values from -0.044194174 to 1.5
- damping: float32 [4, 128], P('region'), may hold values from 0.1 to 0.25
- occupation: float32 [8, 4], P('energy', 'region'), may hold values from 0.05 to 0.95
- block_sizes: int32 [4], P('region'), may hold values from 64 to 128
- offsets: int32 [8], replicated, may hold values from -4 to 4
Outputs:
- pol: float32 [2, 8, 4, 96, 128], P(None, 'energy', 'region')
The draws below stay inside these ranges and needn't reach their ends.
All inputs are finite; a program needn't handle non-finite values.
Results may differ from the reference program's by a relative error of at most 0.00085.
Values may be sent and summed in bfloat16 or wider, within the bound.
A program may use at most 64 MiB of HBM per device.

```python
import math
import jax
import jax.numpy as jnp
from jax import lax

ORB = 128
BAND = 96
NB = 4
NE = 8
NK = 8


def draw_coupling(key, part):
    bound_value = 0.5 / ORB ** 0.5
    full_shape = (NB, 2, ORB, ORB)
    random_part = jax.random.uniform(jax.random.fold_in(key, 301), full_shape, jnp.float32, minval=-bound_value, maxval=bound_value)
    strengths = jax.random.uniform(jax.random.fold_in(key, 302), (NB, ORB), jnp.float32, minval=0.5, maxval=1.5)
    unit_diag = jnp.eye(ORB, dtype=jnp.float32)
    real_part = random_part[:, 0] * (1.0 - unit_diag) + strengths[:, :, None] * unit_diag
    return jnp.stack([real_part, random_part[:, 1]], axis=1).astype(jnp.float32)


def draw_block_sizes(key, part):
    drawn_values = jax.random.randint(jax.random.fold_in(key, 101), (NB,), ORB // 2, ORB + 1)
    ordering = jax.random.permutation(jax.random.fold_in(key, 102), NB)
    places = jnp.arange(NB)
    drawn_values = jnp.where(places == ordering[0], ORB, drawn_values)
    drawn_values = jnp.where(places == ordering[1], ORB // 2, drawn_values)
    return drawn_values.astype(jnp.int32)


def draw_offsets(key, part):
    half_range = NE // 2
    drawn_values = jax.random.randint(jax.random.fold_in(key, 201), (NK,), -half_range, half_range + 1)
    ordering = jax.random.permutation(jax.random.fold_in(key, 202), NK)
    places = jnp.arange(NK)
    drawn_values = jnp.where(places == ordering[0], half_range, drawn_values)
    drawn_values = jnp.where(places == ordering[1], -half_range, drawn_values)
    return drawn_values.astype(jnp.int32)


def levels(key, shape, cuts, low, largest):
    level, own = 1.0, jax.random.fold_in(key, 6)
    for axis_at, blocks in cuts:
        heights = jnp.exp(jax.random.uniform(jax.random.fold_in(own, axis_at), (blocks,), jnp.float32, low / len(cuts), largest / len(cuts)))
        level = level * jnp.repeat(heights, shape[axis_at] // blocks).reshape([-1 if axis == axis_at else 1 for axis in range(len(shape))])
    return level


def scatter_about(stream_key, dims, width, limit, cuts=(), kind=jnp.bfloat16):
    level = levels(stream_key, dims, cuts, -0.22, 0.18) if cuts else 1.0
    values = jax.random.normal(stream_key, dims, jnp.float32) * width * level
    return jnp.minimum(jnp.maximum(values, -limit), limit).astype(kind)


def setup_inputs(seed: int = 0) -> dict:
    splits = jax.random.split(jax.random.key(seed), 7)
    onsite = scatter_about(splits[0], (NB, 2, ORB, ORB), ORB ** -0.5, 0.5, ((0, 4),), jnp.float32)
    coupling = draw_coupling(jax.random.fold_in(splits[6], 71), 0)
    damping = jnp.clip(jnp.exp(math.log(0.25) - 0.9162907 * jax.random.uniform(splits[2], (NB, ORB), jnp.float32) ** levels(splits[2], (NB, ORB), ((0, 4),), -0.2, 0.2)), 0.1, 0.25)
    occupation = jnp.clip(0.05 + 0.9 * jax.random.uniform(splits[3], (NE, NB), jnp.float32) ** levels(splits[3], (NE, NB), ((0, 8), (1, 4)), -0.2, 0.2), 0.05, 0.95)
    block_sizes = draw_block_sizes(jax.random.fold_in(splits[6], 71), 0)
    offsets = draw_offsets(jax.random.fold_in(splits[6], 71), 0)
    return dict(onsite=onsite, coupling=coupling, damping=damping, occupation=occupation, block_sizes=block_sizes, offsets=offsets)


energy_step = 0.1
left_lead = 0.5

def product(former, latter):
    return jnp.matmul(former, latter, precision=lax.Precision.HIGHEST)

def complex_mul(former, latter):
    return (product(former[0], latter[0]) - product(former[1], latter[1]), product(former[0], latter[1]) + product(former[1], latter[0]))

def complex_add(former, latter):
    return (former[0] + latter[0], former[1] + latter[1])

def complex_sub(former, latter):
    return (former[0] - latter[0], former[1] - latter[1])

def adjoint(matrix):
    return (jnp.swapaxes(matrix[0], -1, -2), -jnp.swapaxes(matrix[1], -1, -2))

def normal_solve(matrix, projected):
    orbitals = matrix[0].shape[-1]
    gram_re, gram_im = complex_mul(adjoint(matrix), matrix)
    top_rows = jnp.concatenate([gram_re, -gram_im], axis=-1)
    low_rows = jnp.concatenate([gram_im, gram_re], axis=-1)
    factor = jnp.linalg.cholesky(jnp.concatenate([top_rows, low_rows], axis=-2))
    stacked = jnp.concatenate([projected[0], projected[1]], axis=-2)
    halfway = jax.scipy.linalg.solve_triangular(factor, stacked, lower=True)
    solution = jax.scipy.linalg.solve_triangular(factor, halfway, lower=True, trans=1)
    return (solution[..., :orbitals, :], solution[..., orbitals:, :])

def inverse(matrix):
    return normal_solve(matrix, adjoint(matrix))

def slab_setup(onsite, coupling, damping, block_sizes):
    orbitals = onsite.shape[-1]
    orbital = jnp.arange(orbitals, dtype=jnp.int32)
    active = (orbital[None, :] < block_sizes[:, None]).astype(jnp.float32)
    outer_mask = active[:, :, None] * active[:, None, :]
    ham_re = 0.5 * (onsite[:, 0] + jnp.swapaxes(onsite[:, 0], -1, -2)) * outer_mask
    ham_im = 0.5 * (onsite[:, 1] - jnp.swapaxes(onsite[:, 1], -1, -2)) * outer_mask
    couplings = (coupling[:, 0] * outer_mask, coupling[:, 1] * outer_mask)
    unit_matrix = jnp.eye(orbitals, dtype=jnp.float32)
    base_re = -ham_re
    base_im = damping[:, :, None] * unit_matrix - ham_im
    return (base_re, base_im, couplings)

def band_parts(green_fn, block_sizes, occupied, band_width):
    orbitals = green_fn[0].shape[-1]
    spec_re = -(green_fn[1] + jnp.swapaxes(green_fn[1], -1, -2))
    spec_im = green_fn[0] - jnp.swapaxes(green_fn[0], -1, -2)

    def skewed(matrix):
        lead_shape = matrix.shape[:-2]
        flat_rows = matrix.reshape(lead_shape + (orbitals * orbitals,))
        padded = jnp.concatenate([flat_rows, jnp.zeros(lead_shape + (orbitals,), matrix.dtype)], axis=-1)
        kept = padded.reshape(lead_shape + (orbitals, orbitals + 1))[..., :band_width]
        return jnp.swapaxes(kept, -1, -2)
    reach = jnp.arange(band_width, dtype=jnp.int32)[:, None] + jnp.arange(orbitals, dtype=jnp.int32)[None, :]
    valid_mask = (reach[None] < block_sizes[:, None, None]).astype(jnp.float32)
    band_re = skewed(spec_re) * valid_mask
    band_im = skewed(spec_im) * valid_mask
    weight = occupied[..., None, None]
    return jnp.stack([weight * band_re, weight * band_im, (1.0 - weight) * band_re, (1.0 - weight) * band_im]).astype(jnp.bfloat16)

def reference(onsite, coupling, damping, occupation, block_sizes, offsets):
    orbitals = onsite.shape[-1]
    total_energies = occupation.shape[0]
    unit_matrix = jnp.eye(orbitals, dtype=jnp.float32)
    base_re, base_im, couplings = slab_setup(onsite, coupling, damping, block_sizes)
    last_link = (couplings[0][-1], couplings[1][-1])
    lead_re, lead_im = complex_mul(last_link, adjoint(last_link))
    base_re = base_re.at[-1].add(-lead_im)
    base_im = base_im.at[-1].add(lead_re)
    base_im = base_im.at[0].add(left_lead * unit_matrix)
    numbers = jnp.arange(total_energies, dtype=jnp.int32) - total_energies // 2
    energies = energy_step * numbers.astype(jnp.float32)
    zero_pair = (jnp.zeros((orbitals, orbitals), jnp.float32), jnp.zeros((orbitals, orbitals), jnp.float32))

    def one_energy(inputs):
        energy, occupied = inputs

        def forward(self_energy, slab_data):
            a_re, a_im, link_re, link_im = slab_data
            slab_matrix = (a_re + energy * unit_matrix, a_im)
            green_fn = inverse(complex_sub(slab_matrix, self_energy))
            link_pair = (link_re, link_im)
            next_self = complex_mul(complex_mul(adjoint(link_pair), green_fn), link_pair)
            return (next_self, green_fn)
        unused, left_green = lax.scan(forward, zero_pair, (base_re, base_im, couplings[0], couplings[1]))

        def backward(after_fn, slab_data):
            g_re, g_im, link_re, link_im = slab_data
            green_fn = (g_re, g_im)
            link_pair = (link_re, link_im)
            full_green = complex_add(green_fn, complex_mul(complex_mul(complex_mul(green_fn, link_pair), after_fn), complex_mul(adjoint(link_pair), green_fn)))
            return (full_green, full_green)
        unused, full_green = lax.scan(backward, zero_pair, (left_green[0], left_green[1], couplings[0], couplings[1]), reverse=True)
        return band_parts(full_green, block_sizes, occupied, BAND)
    band_data = lax.map(one_energy, (energies, occupation)).astype(jnp.float32)
    less_re, less_im = (band_data[:, 0], band_data[:, 1])
    great_re, great_im = (band_data[:, 2], band_data[:, 3])
    zeros_pad = jnp.zeros_like(great_re)
    pad_re = jnp.concatenate([zeros_pad, great_re, zeros_pad], axis=0)
    pad_im = jnp.concatenate([zeros_pad, great_im, zeros_pad], axis=0)

    def one_offset(offset):
        initial = (total_energies - offset).astype(jnp.int32)
        shift_re = lax.dynamic_slice_in_dim(pad_re, initial, total_energies, 0)
        shift_im = lax.dynamic_slice_in_dim(pad_im, initial, total_energies, 0)
        pol_re = energy_step * jnp.sum(less_re * shift_re + less_im * shift_im, axis=0)
        pol_im = energy_step * jnp.sum(less_im * shift_re - less_re * shift_im, axis=0)
        return jnp.stack([pol_re, pol_im])
    result = lax.map(one_offset, offsets)
    return jnp.swapaxes(result, 0, 1)
```

```python
import functools
import jax
import jax.numpy as jnp
from jax import lax
from jax.experimental import pallas as pl
from jax.experimental.pallas import tpu as pltpu
from jax.sharding import PartitionSpec as P

BAND = 96
PANEL = 8

energy_step = 0.1
left_lead = 0.5

VM = pl.BlockSpec(memory_space=pltpu.VMEM)
SM = pl.BlockSpec(memory_space=pltpu.SMEM)


def dot(x, y):
    return jnp.dot(x, y, precision=lax.Precision.HIGHEST, preferred_element_type=jnp.float32)


def halves(x):
    n = x.shape[-1] // 2
    return x[:, :n], x[:, n:]


def cat(re, im):
    return jnp.concatenate([re, im], axis=1)


def adjoint(x):
    re, im = halves(x)
    return cat(re.T, -im.T)


def cmul(x, y):
    re, im = halves(y)
    return dot(x, jnp.concatenate([y, cat(-im, re)], axis=0))


def lane_bcast(x, j):
    return jnp.broadcast_to(x[:, j : j + 1], x.shape)


def row_bcast(x, k):
    return jnp.broadcast_to(x[k : k + 1, :], x.shape)


def invert(a, rhs):
    n = a.shape[0]
    rhs[...] = jnp.zeros_like(rhs)
    lane = lax.broadcasted_iota(jnp.int32, (PANEL, n), 1)
    sub = lax.broadcasted_iota(jnp.int32, (PANEL, n), 0)
    wide = lax.broadcasted_iota(jnp.int32, (n, 2 * n), 1) % n

    def block(b, carry):
        start = pl.multiple_of(b * PANEL, PANEL)
        rows = pl.ds(start, PANEL)
        x = a[rows, :]
        xr, xi = halves(x)
        turn = (n - start) % n
        tr = pltpu.roll(xr, turn, 1)
        ti = pltpu.roll(xi, turn, 1)
        cols = [(lane_bcast(tr, j), lane_bcast(ti, j)) for j in range(PANEL)]
        inside = (lane >= start) & (lane < start + PANEL)
        cols.append(
            (
                jnp.where(inside, (lane - start == sub).astype(jnp.float32), xr),
                jnp.where(inside, 0.0, xi),
            )
        )
        for k in range(PANEL):
            br, bi = cols[k]
            pr, pi = row_bcast(br, k), row_bcast(bi, k)
            scale = 1.0 / (pr * pr + pi * pi)
            ir, ii = pr * scale, -pi * scale
            here = sub == k
            mr = jnp.where(here, -ir, br * ir - bi * ii)
            mi = jnp.where(here, -ii, br * ii + bi * ir)
            for j in range(k + 1, PANEL + 1):
                cr, ci = cols[j]
                rr, ri = row_bcast(cr, k), row_bcast(ci, k)
                cols[j] = (
                    jnp.where(here, 0.0, cr) - (mr * rr - mi * ri),
                    jnp.where(here, 0.0, ci) - (mr * ri + mi * rr),
                )
        zr, zi = cols[PANEL]
        low = pl.ds(pl.multiple_of(n + start, PANEL), PANEL)
        rhs[rows, :] = cat(zr, zi)
        rhs[low, :] = cat(-zi, zr)
        old = a[...]
        keep = (wide < start) | (wide >= start + PANEL)
        a[...] = jnp.where(keep, old, 0.0) - dot(old, rhs[...])
        a[rows, :] = cat(zr, zi)
        rhs[rows, :] = jnp.zeros((PANEL, 2 * n), jnp.float32)
        rhs[low, :] = jnp.zeros((PANEL, 2 * n), jnp.float32)
        return carry

    lax.fori_loop(0, n // PANEL, block, 0)


def build(regions, total, size, onsite, coupling, damping):
    n = onsite.shape[-1]
    row = lax.broadcasted_iota(jnp.int32, (n, n), 0)
    col = lax.broadcasted_iota(jnp.int32, (n, n), 1)
    mask = ((row < size) & (col < size)).astype(jnp.float32)
    eye = row == col
    region = lax.axis_index("region")
    energy = energy_step * (lax.axis_index("energy") - total // 2).astype(jnp.float32)
    o_re, o_im = onsite[0, 0], onsite[0, 1]
    h_re = 0.5 * (o_re + o_re.T) * mask
    h_im = 0.5 * (o_im - o_im.T) * mask
    u = cat(coupling[0, 0] * mask, coupling[0, 1] * mask)
    diag_im = jnp.broadcast_to(damping[...], (n, n)) + jnp.where(region == 0, left_lead, 0.0)
    a_re = jnp.where(eye, energy, 0.0) - h_re
    a_im = jnp.where(eye, diag_im, 0.0) - h_im
    return cat(a_re, a_im), u


def build_kernel(regions, total, sizes, onsite, coupling, damping, a_ref, u_ref):
    a, u = build(regions, total, sizes[0], onsite, coupling, damping)
    u_ref[...] = u
    a_ref[...] = a

    @pl.when(lax.axis_index("region") == regions - 1)
    def _():
        l_re, l_im = halves(cmul(u, adjoint(u)))
        a_ref[...] = a + cat(-l_im, l_re)


def step_kernel(a_ref, s_ref, w_ref, g_ref, out_ref, rhs):
    g_ref[...] = a_ref[...] - s_ref[...]
    invert(g_ref, rhs)
    w = w_ref[...]
    out_ref[...] = cmul(cmul(adjoint(w), g_ref[...]), w)


def back_kernel(g_ref, w_ref, after_ref, out_ref):
    g, w = g_ref[...], w_ref[...]
    out_ref[...] = g + cmul(cmul(cmul(g, w), after_ref[...]), cmul(adjoint(w), g))


def skew(t):
    n = t.shape[0]
    col = lax.broadcasted_iota(jnp.int32, (n, n), 1)
    bit = 1
    while bit < n:
        moved = jnp.concatenate([t[bit:], t[:bit]], axis=0)
        t = jnp.where((col // bit) % 2 == 1, moved, t)
        bit *= 2
    return t


def band_values(g, size, weight):
    re, im = halves(g)
    t_re = -(im + im.T)
    t_im = re.T - re
    n = re.shape[0]
    row = lax.broadcasted_iota(jnp.int32, (BAND, n), 0)
    col = lax.broadcasted_iota(jnp.int32, (BAND, n), 1)
    valid = (row + col < size).astype(jnp.float32)
    b_re = skew(t_re)[:BAND] * valid
    b_im = skew(t_im)[:BAND] * valid
    return [
        (weight * b_re),
        (weight * b_im),
        ((1.0 - weight) * b_re),
        ((1.0 - weight) * b_im),
    ]


def band_kernel(sizes, occ, g_ref, out_ref):
    count, rows = out_ref.shape[1], out_ref.shape[2]
    for c, v in enumerate(band_values(g_ref[...], sizes[0], occ[0, 0])):
        for e in range(count):
            out_ref[c, e] = v[e * rows : (e + 1) * rows].astype(jnp.bfloat16)


def pol_kernel(offsets, v_ref, out_ref):
    total = v_ref.shape[1]

    def one(k, carry):
        shape = v_ref.shape[2:]

        def term(e, acc):
            m = e - offsets[k]
            on = jnp.where((m >= 0) & (m < total), 1.0, 0.0)
            m = jnp.clip(m, 0, total - 1)
            lr = v_ref[0, e].astype(jnp.float32)
            li = v_ref[1, e].astype(jnp.float32)
            gr = v_ref[2, m].astype(jnp.float32) * on
            gi = v_ref[3, m].astype(jnp.float32) * on
            return (acc[0] + (lr * gr + li * gi), acc[1] + (li * gr - lr * gi))

        zero = jnp.zeros(shape, jnp.float32)
        re, im = lax.fori_loop(0, total, term, (zero, zero))
        out_ref[k, 0] = energy_step * re
        out_ref[k, 1] = energy_step * im
        return carry

    lax.fori_loop(0, out_ref.shape[0], one, 0)


def f32(*shape):
    return jax.ShapeDtypeStruct(shape, jnp.float32)


def local(onsite, coupling, damping, occupation, block_sizes, offsets):
    n = onsite.shape[-1]
    regions = lax.axis_size("region")
    total = lax.axis_size("energy")
    half = regions // 2
    pos = lax.axis_index("region")
    left = pos < half
    rows = BAND // total
    a, u = pl.pallas_call(
        functools.partial(build_kernel, regions, total),
        in_specs=[SM, VM, VM, VM],
        out_specs=[VM, VM],
        out_shape=[f32(n, 2 * n), f32(n, 2 * n)],
    )(block_sizes, onsite, coupling, damping)
    lower = lax.ppermute(u, "region", [(r, r + 1) for r in range(half - 1, regions - 1)])
    w = jnp.where(left, u, adjoint(lower))
    step = pl.pallas_call(
        step_kernel,
        in_specs=[VM, VM, VM],
        out_specs=[VM, VM],
        out_shape=[f32(n, 2 * n), f32(n, 2 * n)],
        scratch_shapes=[pltpu.VMEM((2 * n, 2 * n), jnp.float32)],
    )
    inward = [(r, r + 1) for r in range(half - 1)] + [(r, r - 1) for r in range(half + 1, regions)]
    sigma = jnp.zeros((n, 2 * n), jnp.float32)
    for s in range(half):
        g, out = step(a, sigma, w)
        if s < half - 1:
            sigma = lax.ppermute(out, "region", inward)
    middle = lax.ppermute(out, "region", [(half - 1, half), (half, half - 1)])
    full, _ = step(a, sigma + middle, w)
    outward = [(d, s) for s, d in inward]
    mid = (pos == half - 1) | (pos == half)
    back = pl.pallas_call(
        back_kernel, in_specs=[VM] * 3, out_specs=VM, out_shape=f32(n, 2 * n)
    )
    for s in range(half - 1):
        after = lax.ppermute(full, "region", outward)
        full = jnp.where(mid, full, back(g, w, after))
    packed = pl.pallas_call(
        band_kernel,
        in_specs=[SM, SM, VM],
        out_specs=VM,
        out_shape=jax.ShapeDtypeStruct((4, total, rows, n), jnp.bfloat16),
    )(block_sizes, occupation, full)
    moved = lax.all_to_all(packed, "energy", split_axis=1, concat_axis=1, tiled=True)
    freq = offsets.shape[0]
    res = pl.pallas_call(
        pol_kernel, in_specs=[SM, VM], out_specs=VM, out_shape=f32(freq, 2, rows, n)
    )(offsets, moved)
    res = lax.all_to_all(res, "energy", split_axis=0, concat_axis=0, tiled=True)
    res = res.reshape(total, freq // total, 2, rows, n)
    res = jnp.transpose(res, (2, 1, 0, 3, 4))
    return res.reshape(2, freq // total, 1, BAND, n)


def solution(mesh):
    placed = (
        P("region", None, None, None),
        P("region", None, None, None),
        P("region", None),
        P("energy", "region"),
        P("region"),
        P(),
    )
    return jax.shard_map(
        local,
        mesh=mesh,
        in_specs=placed,
        out_specs=P(None, "energy", "region", None, None),
        check_vma=False,
    )
```

```python
import functools
import jax
import jax.numpy as jnp
from jax import lax
from jax.experimental import pallas as pl
from jax.experimental.pallas import tpu as pltpu
from jax.sharding import PartitionSpec as P

BAND = 96
PANEL = 8

energy_step = 0.1
left_lead = 0.5

VM = pl.BlockSpec(memory_space=pltpu.VMEM)
SM = pl.BlockSpec(memory_space=pltpu.SMEM)


def dot(x, y):
    return jnp.dot(x, y, precision=lax.Precision.HIGHEST, preferred_element_type=jnp.float32)


def halves(x):
    n = x.shape[-1] // 2
    return x[:, :n], x[:, n:]


def cat(re, im):
    return jnp.concatenate([re, im], axis=1)


def adjoint(x):
    re, im = halves(x)
    return cat(re.T, -im.T)


def cmul(x, y):
    re, im = halves(y)
    return dot(x, jnp.concatenate([y, cat(-im, re)], axis=0))


def lane_bcast(x, j):
    return jnp.broadcast_to(x[:, j : j + 1], x.shape)


def row_bcast(x, k):
    return jnp.broadcast_to(x[k : k + 1, :], x.shape)


def invert(a, rhs):
    n = a.shape[0]
    rhs[...] = jnp.zeros_like(rhs)
    lane = lax.broadcasted_iota(jnp.int32, (PANEL, n), 1)
    sub = lax.broadcasted_iota(jnp.int32, (PANEL, n), 0)
    wide = lax.broadcasted_iota(jnp.int32, (n, 2 * n), 1) % n

    def block(b, carry):
        start = pl.multiple_of(b * PANEL, PANEL)
        rows = pl.ds(start, PANEL)
        x = a[rows, :]
        xr, xi = halves(x)
        turn = (n - start) % n
        tr = pltpu.roll(xr, turn, 1)
        ti = pltpu.roll(xi, turn, 1)
        cols = [(lane_bcast(tr, j), lane_bcast(ti, j)) for j in range(PANEL)]
        inside = (lane >= start) & (lane < start + PANEL)
        cols.append(
            (
                jnp.where(inside, (lane - start == sub).astype(jnp.float32), xr),
                jnp.where(inside, 0.0, xi),
            )
        )
        for k in range(PANEL):
            br, bi = cols[k]
            pr, pi = row_bcast(br, k), row_bcast(bi, k)
            scale = 1.0 / (pr * pr + pi * pi)
            ir, ii = pr * scale, -pi * scale
            here = sub == k
            mr = jnp.where(here, -ir, br * ir - bi * ii)
            mi = jnp.where(here, -ii, br * ii + bi * ir)
            for j in range(k + 1, PANEL + 1):
                cr, ci = cols[j]
                rr, ri = row_bcast(cr, k), row_bcast(ci, k)
                cols[j] = (
                    jnp.where(here, 0.0, cr) - (mr * rr - mi * ri),
                    jnp.where(here, 0.0, ci) - (mr * ri + mi * rr),
                )
        zr, zi = cols[PANEL]
        low = pl.ds(pl.multiple_of(n + start, PANEL), PANEL)
        rhs[rows, :] = cat(zr, zi)
        rhs[low, :] = cat(-zi, zr)
        old = a[...]
        keep = (wide < start) | (wide >= start + PANEL)
        a[...] = jnp.where(keep, old, 0.0) - dot(old, rhs[...])
        a[rows, :] = cat(zr, zi)
        rhs[rows, :] = jnp.zeros((PANEL, 2 * n), jnp.float32)
        rhs[low, :] = jnp.zeros((PANEL, 2 * n), jnp.float32)
        return carry

    lax.fori_loop(0, n // PANEL, block, 0)


def build(regions, total, size, onsite, coupling, damping):
    n = onsite.shape[-1]
    row = lax.broadcasted_iota(jnp.int32, (n, n), 0)
    col = lax.broadcasted_iota(jnp.int32, (n, n), 1)
    mask = ((row < size) & (col < size)).astype(jnp.float32)
    eye = row == col
    region = lax.axis_index("region")
    energy = energy_step * (lax.axis_index("energy") - total // 2).astype(jnp.float32)
    o_re, o_im = onsite[0, 0], onsite[0, 1]
    h_re = 0.5 * (o_re + o_re.T) * mask
    h_im = 0.5 * (o_im - o_im.T) * mask
    u = cat(coupling[0, 0] * mask, coupling[0, 1] * mask)
    diag_im = jnp.broadcast_to(damping[...], (n, n)) + jnp.where(region == 0, left_lead, 0.0)
    a_re = jnp.where(eye, energy, 0.0) - h_re
    a_im = jnp.where(eye, diag_im, 0.0) - h_im
    return cat(a_re, a_im), u


def skew(t):
    n = t.shape[0]
    col = lax.broadcasted_iota(jnp.int32, (n, n), 1)
    bit = 1
    while bit < n:
        moved = jnp.concatenate([t[bit:], t[:bit]], axis=0)
        t = jnp.where((col // bit) % 2 == 1, moved, t)
        bit *= 2
    return t


def band_values(g, size, weight):
    re, im = halves(g)
    t_re = -(im + im.T)
    t_im = re.T - re
    n = re.shape[0]
    row = lax.broadcasted_iota(jnp.int32, (BAND, n), 0)
    col = lax.broadcasted_iota(jnp.int32, (BAND, n), 1)
    valid = (row + col < size).astype(jnp.float32)
    b_re = skew(t_re)[:BAND] * valid
    b_im = skew(t_im)[:BAND] * valid
    return [
        (weight * b_re),
        (weight * b_im),
        ((1.0 - weight) * b_re),
        ((1.0 - weight) * b_im),
    ]


def send(src, dst, sems, axis, index):
    return pltpu.make_async_remote_copy(
        src_ref=src,
        dst_ref=dst,
        send_sem=sems[0],
        recv_sem=sems[1],
        device_id={axis: index},
        device_id_type=pl.DeviceIdType.MESH,
    )


def kernel(
    regions, peers, sizes, occ, offsets, onsite, coupling, damping, out_ref,
    a, g, w, u, u_in, s_out, s_in, m_out, m_in, g_in, full, rhs,
    band_out, band_in, pol_out, pol_in,
    link_send, link_recv, band_send, band_recv, pol_send, pol_recv,
):
    half = regions // 2
    pos = lax.axis_index("region")
    me = lax.axis_index("energy")
    left = pos < half
    inner = jnp.where(left, pos + 1, pos - 1)
    outer = jnp.where(left, pos - 1, pos + 1)
    is_mid = (pos == half - 1) | (pos == half)
    is_end = (pos == 0) | (pos == regions - 1)

    barrier = pltpu.get_barrier_semaphore()

    def greet(axis, index):
        pl.semaphore_signal(
            barrier, inc=1, device_id={axis: index}, device_id_type=pl.DeviceIdType.MESH
        )

    greet("region", inner)

    @pl.when(jnp.logical_not(is_end))
    def _():
        greet("region", outer)

    def greet_peer(j, carry):
        greet("energy", lax.rem(me + j, peers))
        return carry

    lax.fori_loop(1, peers, greet_peer, 0)

    a0, u0 = build(regions, peers, sizes[0], onsite, coupling, damping)
    u[...] = u0
    w[...] = u0
    a[...] = a0

    @pl.when(is_end)
    def _():
        pl.semaphore_wait(barrier, peers)

    @pl.when(jnp.logical_not(is_end))
    def _():
        pl.semaphore_wait(barrier, peers + 1)

    def link(i, src, dst, index):
        return send(src, dst, (link_send.at[i], link_recv.at[i]), "region", index)

    gives = (pos >= half - 1) & (pos < regions - 1)

    @pl.when(gives)
    def _():
        link(0, u, u_in, pos + 1).start()

    @pl.when(pos == regions - 1)
    def _():
        l_re, l_im = halves(cmul(u0, adjoint(u0)))
        a[...] = a0 + cat(-l_im, l_re)

    @pl.when(jnp.logical_not(is_end))
    def _():
        link(1, s_out, s_in, outer).wait_recv()
        a[...] = a[...] - s_in[...]

    g[...] = a[...]
    invert(g, rhs)

    @pl.when(jnp.logical_not(left))
    def _():
        link(0, u, u_in, pos - 1).wait_recv()
        w[...] = adjoint(u_in[...])

    @pl.when(is_mid)
    def _():
        wv = w[...]
        m_out[...] = cmul(cmul(adjoint(wv), g[...]), wv)
        copy = link(2, m_out, m_in, inner)
        copy.start()
        copy.wait_recv()
        full[...] = a[...] - m_in[...]
        invert(full, rhs)
        copy.wait_send()

    @pl.when(jnp.logical_not(is_mid))
    def _():
        wv = w[...]
        wg = cmul(adjoint(wv), g[...])
        s_out[...] = cmul(wg, wv)
        copy = link(1, s_out, s_in, inner)
        copy.start()
        gw = cmul(g[...], wv)
        link(3, full, g_in, inner).wait_recv()
        full[...] = g[...] + cmul(cmul(gw, g_in[...]), wg)
        copy.wait_send()

    @pl.when(jnp.logical_not(is_end))
    def _():
        link(3, full, g_in, outer).start()

    rows = BAND // peers
    n = onsite.shape[-1]
    for c, v in enumerate(band_values(full[...], sizes[0], occ[0, 0])):
        v = v.astype(jnp.bfloat16)
        for e in range(peers):
            band_out[e, c] = v[e * rows : (e + 1) * rows]

    def band_copy(j):
        peer = lax.rem(me + j, peers)
        return send(
            band_out.at[peer], band_in.at[me], (band_send.at[j], band_recv.at[j]), "energy", peer
        )

    def each(make, act):
        def one(j, carry):
            act(make(j))
            return carry

        lax.fori_loop(1, peers, one, 0)

    each(band_copy, lambda c: c.start())
    band_in[me] = band_out[me]
    each(band_copy, lambda c: c.wait_recv())

    kept = offsets.shape[0] // peers

    def pol_copy(j):
        peer = lax.rem(me + j, peers)
        return send(
            pol_out.at[peer], pol_in.at[me], (pol_send.at[j], pol_recv.at[j]), "energy", peer
        )

    def frequency(owner, i):
        offset = offsets[owner * kept + i]

        def term(e, acc):
            m = e - offset
            on = jnp.where((m >= 0) & (m < peers), 1.0, 0.0)
            m = jnp.clip(m, 0, peers - 1)
            lr = band_in[e, 0].astype(jnp.float32)
            li = band_in[e, 1].astype(jnp.float32)
            gr = band_in[m, 2].astype(jnp.float32) * on
            gi = band_in[m, 3].astype(jnp.float32) * on
            return (acc[0] + (lr * gr + li * gi), acc[1] + (li * gr - lr * gi))

        acc = (jnp.zeros((rows, n), jnp.float32), jnp.zeros((rows, n), jnp.float32))
        if peers <= 16:
            for e in range(peers):
                acc = term(e, acc)
        else:
            acc = lax.fori_loop(0, peers, term, acc)
        return energy_step * acc[0], energy_step * acc[1]

    def owned(j, carry):
        owner = lax.rem(me + j, peers)
        for i in range(kept):
            re, im = frequency(owner, i)
            pol_out[owner, i, 0] = re
            pol_out[owner, i, 1] = im

        pol_copy(j).start()
        return carry

    lax.fori_loop(1, peers, owned, 0)
    for i in range(kept):
        re, im = frequency(me, i)
        pol_in[me, i, 0] = re
        pol_in[me, i, 1] = im
    each(pol_copy, lambda c: c.wait_recv())
    for e in range(peers):
        for i in range(kept):
            for c in range(2):
                out_ref[c, i, 0, e * rows : (e + 1) * rows, :] = pol_in[e, i, c]

    each(band_copy, lambda c: c.wait_send())
    each(pol_copy, lambda c: c.wait_send())

    @pl.when(gives)
    def _():
        link(0, u, u_in, pos + 1).wait_send()

    @pl.when(jnp.logical_not(is_end))
    def _():
        link(3, full, g_in, outer).wait_send()


def local(onsite, coupling, damping, occupation, block_sizes, offsets):
    n = onsite.shape[-1]
    regions = lax.axis_size("region")
    peers = lax.axis_size("energy")
    rows = BAND // peers
    kept = offsets.shape[0] // peers
    block = pltpu.VMEM((n, 2 * n), jnp.float32)
    return pl.pallas_call(
        functools.partial(kernel, regions, peers),
        in_specs=[SM, SM, SM, VM, VM, VM],
        out_specs=VM,
        out_shape=jax.ShapeDtypeStruct((2, kept, 1, BAND, n), jnp.float32),
        scratch_shapes=[block] * 11
        + [
            pltpu.VMEM((2 * n, 2 * n), jnp.float32),
            pltpu.VMEM((peers, 4, rows, n), jnp.bfloat16),
            pltpu.VMEM((peers, 4, rows, n), jnp.bfloat16),
            pltpu.VMEM((peers, kept, 2, rows, n), jnp.float32),
            pltpu.VMEM((peers, kept, 2, rows, n), jnp.float32),
            pltpu.SemaphoreType.DMA((4,)),
            pltpu.SemaphoreType.DMA((4,)),
        ]
        + [pltpu.SemaphoreType.DMA((peers,))] * 4,
        compiler_params=pltpu.CompilerParams(collective_id=0, has_side_effects=True),
    )(block_sizes, occupation, offsets, onsite, coupling, damping)


def solution(mesh):
    placed = (
        P("region", None, None, None),
        P("region", None, None, None),
        P("region", None),
        P("energy", "region"),
        P("region"),
        P(),
    )
    return jax.shard_map(
        local,
        mesh=mesh,
        in_specs=placed,
        out_specs=P(None, "energy", "region", None, None),
        check_vma=False,
    )
```

```python
import functools
import jax
import jax.numpy as jnp
from jax import lax
from jax.experimental import pallas as pl
from jax.experimental.pallas import tpu as pltpu
from jax.sharding import PartitionSpec as P

BAND = 96
PANEL = 8

energy_step = 0.1
left_lead = 0.5

VM = pl.BlockSpec(memory_space=pltpu.VMEM)
SM = pl.BlockSpec(memory_space=pltpu.SMEM)


def dot(x, y):
    return jnp.dot(x, y, precision=lax.Precision.HIGHEST, preferred_element_type=jnp.float32)


def halves(x):
    n = x.shape[-1] // 2
    return x[:, :n], x[:, n:]


def cat(re, im):
    return jnp.concatenate([re, im], axis=1)


def adjoint(x):
    re, im = halves(x)
    return cat(re.T, -im.T)


def cmul(x, y):
    re, im = halves(y)
    return dot(x, jnp.concatenate([y, cat(-im, re)], axis=0))


def lane_bcast(x, j):
    return jnp.broadcast_to(x[:, j : j + 1], x.shape)


def row_bcast(x, k):
    return jnp.broadcast_to(x[k : k + 1, :], x.shape)


def factor(x, start):
    xr, xi = x
    n = xr.shape[1]
    lane = lax.broadcasted_iota(jnp.int32, (PANEL, n), 1) - start
    sub = lax.broadcasted_iota(jnp.int32, (PANEL, n), 0)
    turn = (n - start) % n
    tr = pltpu.roll(xr, turn, 1)
    ti = pltpu.roll(xi, turn, 1)
    cols = [(lane_bcast(tr, j), lane_bcast(ti, j)) for j in range(PANEL)]
    inside = (lane >= 0) & (lane < PANEL)
    cols.append((jnp.where(inside, (lane == sub).astype(jnp.float32), xr), jnp.where(inside, 0.0, xi)))
    for k in range(PANEL):
        br, bi = cols[k]
        pr, pi = row_bcast(br, k), row_bcast(bi, k)
        scale = 1.0 / (pr * pr + pi * pi)
        here = sub == k
        qr = jnp.where(here, -pr, br * pr + bi * pi)
        qi = jnp.where(here, pi, bi * pr - br * pi)
        mr, mi = qr * scale, qi * scale
        for j in range(k + 1, PANEL + 1):
            cr, ci = cols[j]
            rr, ri = row_bcast(cr, k), row_bcast(ci, k)
            cols[j] = (
                jnp.where(here, 0.0, cr) - (mr * rr - mi * ri),
                jnp.where(here, 0.0, ci) - (mr * ri + mi * rr),
            )
    return cols[PANEL]

def invert(a, rhs):
    n = a.shape[0]
    rhs[...] = jnp.zeros_like(rhs)
    lane = lax.broadcasted_iota(jnp.int32, (PANEL, n), 1)
    wide = lax.broadcasted_iota(jnp.int32, (n, 2 * n), 1) % n
    zero = jnp.zeros((PANEL, 2 * n), jnp.float32)

    def places(start):
        return pl.ds(start, PANEL), pl.ds(pl.multiple_of(n + start, PANEL), PANEL)

    def put(start, z):
        rows, low = places(start)
        rhs[rows, :] = cat(z[0], z[1])
        rhs[low, :] = cat(-z[1], z[0])

    def updated(start):
        old = a[...]
        keep = (wide < start) | (wide >= start + PANEL)
        return jnp.where(keep, old, 0.0) - dot(old, rhs[...])

    def clear(start):
        rows, low = places(start)
        rhs[rows, :] = zero
        rhs[low, :] = zero

    first = factor(halves(a[:PANEL, :]), 0)
    put(0, first)

    def block(b, z):
        last = pl.multiple_of((b - 1) * PANEL, PANEL)
        start = pl.multiple_of(b * PANEL, PANEL)
        new = updated(last)
        xr, xi = halves(a[pl.ds(start, PANEL), :])
        turn = (n - last) % n
        tr = pltpu.roll(xr, turn, 1)
        ti = pltpu.roll(xi, turn, 1)
        inside = (lane >= last) & (lane < last + PANEL)
        xr = jnp.where(inside, 0.0, xr)
        xi = jnp.where(inside, 0.0, xi)
        accs=[]
        for j in range(PANEL):
            cr, ci = lane_bcast(tr, j), lane_bcast(ti, j)
            rr, ri = row_bcast(z[0], j), row_bcast(z[1], j)
            accs.append((cr * rr - ci * ri, cr * ri + ci * rr))
        while len(accs)>1:
            accs=[(p[0]+q[0],p[1]+q[1]) for p,q in zip(accs[::2],accs[1::2])]
        xr, xi = xr-accs[0][0], xi-accs[0][1]
        fresh = factor((xr, xi), start)
        a[...] = new
        a[pl.ds(last, PANEL), :] = cat(z[0], z[1])
        clear(last)
        put(start, fresh)
        return fresh

    z = lax.fori_loop(1, n // PANEL, block, first)
    last = n - PANEL
    a[...] = updated(last)
    a[pl.ds(last, PANEL), :] = cat(z[0], z[1])


def build(regions, total, size, onsite, coupling, damping):
    n = onsite.shape[-1]
    row = lax.broadcasted_iota(jnp.int32, (n, n), 0)
    col = lax.broadcasted_iota(jnp.int32, (n, n), 1)
    mask = ((row < size) & (col < size)).astype(jnp.float32)
    eye = row == col
    region = lax.axis_index("region")
    energy = energy_step * (lax.axis_index("energy") - total // 2).astype(jnp.float32)
    o_re, o_im = onsite[0, 0], onsite[0, 1]
    h_re = 0.5 * (o_re + o_re.T) * mask
    h_im = 0.5 * (o_im - o_im.T) * mask
    u = cat(coupling[0, 0] * mask, coupling[0, 1] * mask)
    diag_im = jnp.broadcast_to(damping[...], (n, n)) + jnp.where(region == 0, left_lead, 0.0)
    a_re = jnp.where(eye, energy, 0.0) - h_re
    a_im = jnp.where(eye, diag_im, 0.0) - h_im
    return cat(a_re, a_im), u


def skew(t):
    n = t.shape[0]
    col = lax.broadcasted_iota(jnp.int32, (n, n), 1)
    bit = 1
    while bit < n:
        moved = jnp.concatenate([t[bit:], t[:bit]], axis=0)
        t = jnp.where((col // bit) % 2 == 1, moved, t)
        bit *= 2
    return t


def band_values(g, size, weight):
    re, im = halves(g)
    t_re = -(im + im.T)
    t_im = re.T - re
    n = re.shape[0]
    row = lax.broadcasted_iota(jnp.int32, (BAND, n), 0)
    col = lax.broadcasted_iota(jnp.int32, (BAND, n), 1)
    valid = (row + col < size).astype(jnp.float32)
    b_re = skew(t_re)[:BAND] * valid
    b_im = skew(t_im)[:BAND] * valid
    return [
        (weight * b_re),
        (weight * b_im),
        ((1.0 - weight) * b_re),
        ((1.0 - weight) * b_im),
    ]


def send(src, dst, sems, axis, index):
    return pltpu.make_async_remote_copy(
        src_ref=src,
        dst_ref=dst,
        send_sem=sems[0],
        recv_sem=sems[1],
        device_id={axis: index},
        device_id_type=pl.DeviceIdType.MESH,
    )


def kernel(
    regions, peers, sizes, occ, offsets, onsite, coupling, damping, out_ref,
    a, g, w, u, u_in, s_out, s_in, m_out, m_in, g_in, full, rhs,
    band_out, band_in, pol_out, pol_in,
    link_send, link_recv, band_send, band_recv, pol_send, pol_recv,
):
    half = regions // 2
    pos = lax.axis_index("region")
    me = lax.axis_index("energy")
    left = pos < half
    inner = jnp.where(left, pos + 1, pos - 1)
    outer = jnp.where(left, pos - 1, pos + 1)
    is_mid = (pos == half - 1) | (pos == half)
    is_end = (pos == 0) | (pos == regions - 1)

    barrier = pltpu.get_barrier_semaphore()

    def greet(axis, index):
        pl.semaphore_signal(
            barrier, inc=1, device_id={axis: index}, device_id_type=pl.DeviceIdType.MESH
        )

    greet("region", inner)

    @pl.when(jnp.logical_not(is_end))
    def _():
        greet("region", outer)

    def greet_peer(j, carry):
        greet("energy", lax.rem(me + j, peers))
        return carry

    lax.fori_loop(1, peers, greet_peer, 0)

    a0, u0 = build(regions, peers, sizes[0], onsite, coupling, damping)
    u[...] = u0
    w[...] = u0
    a[...] = a0

    gives = (pos >= half - 1) & (pos < regions - 1)
    early = jnp.logical_not(is_end) | gives

    def enter():
        pl.semaphore_wait(barrier, jnp.where(is_end, peers, peers + 1))

    pl.when(early)(enter)

    def link(i, src, dst, index):
        return send(src, dst, (link_send.at[i], link_recv.at[i]), "region", index)

    @pl.when(gives)
    def _():
        link(0, u, u_in, pos + 1).start()

    @pl.when(pos == regions - 1)
    def _():
        l_re, l_im = halves(cmul(u0, adjoint(u0)))
        a[...] = a0 + cat(-l_im, l_re)

    @pl.when(jnp.logical_not(is_end))
    def _():
        link(1, s_out, s_in, outer).wait_recv()

        @pl.when(left)
        def _():
            a[...] = a[...] - s_in[...]

        @pl.when(jnp.logical_not(left))
        def _():
            uv = u[...]
            a[...] = a[...] - cmul(cmul(uv, s_in[...]), adjoint(uv))

    g[...] = a[...]
    invert(g, rhs)
    pl.when(jnp.logical_not(early))(enter)

    own = link(1, s_out, s_in, inner)

    @pl.when(jnp.logical_not(left))
    def _():
        @pl.when(jnp.logical_not(is_mid))
        def _():
            s_out[...] = g[...]
            own.start()

        link(0, u, u_in, pos - 1).wait_recv()
        w[...] = adjoint(u_in[...])

    @pl.when(is_mid)
    def _():
        wv = w[...]
        m_out[...] = cmul(cmul(adjoint(wv), g[...]), wv)
        copy = link(2, m_out, m_in, inner)
        copy.start()
        copy.wait_recv()
        full[...] = a[...] - m_in[...]
        invert(full, rhs)
        copy.wait_send()

    @pl.when(jnp.logical_not(is_mid))
    def _():
        wv = w[...]
        wg = cmul(adjoint(wv), g[...])

        @pl.when(left)
        def _():
            s_out[...] = cmul(wg, wv)
            own.start()

        gw = cmul(g[...], wv)
        link(3, full, g_in, inner).wait_recv()
        full[...] = g[...] + cmul(cmul(gw, g_in[...]), wg)
        own.wait_send()

    @pl.when(jnp.logical_not(is_end))
    def _():
        link(3, full, g_in, outer).start()

    rows = BAND // peers
    n = onsite.shape[-1]
    for c, v in enumerate(band_values(full[...], sizes[0], occ[0, 0])):
        v = v.astype(jnp.bfloat16)
        for e in range(peers):
            band_out[e, c] = v[e * rows : (e + 1) * rows]

    def band_copy(j):
        peer = lax.rem(me + j, peers)
        return send(
            band_out.at[peer], band_in.at[me], (band_send.at[j], band_recv.at[j]), "energy", peer
        )

    def each(make, act):
        def one(j, carry):
            act(make(j))
            return carry

        lax.fori_loop(1, peers, one, 0)

    each(band_copy, lambda c: c.start())
    band_in[me] = band_out[me]
    each(band_copy, lambda c: c.wait_recv())

    kept = offsets.shape[0] // peers

    def pol_copy(j):
        peer = lax.rem(me + j, peers)
        return send(
            pol_out.at[peer], pol_in.at[me], (pol_send.at[j], pol_recv.at[j]), "energy", peer
        )

    def frequency(owner, i):
        offset = offsets[owner * kept + i]

        def term(e, acc):
            m = e - offset
            on = jnp.where((m >= 0) & (m < peers), 1.0, 0.0)
            m = jnp.clip(m, 0, peers - 1)
            lr = band_in[e, 0].astype(jnp.float32)
            li = band_in[e, 1].astype(jnp.float32)
            gr = band_in[m, 2].astype(jnp.float32) * on
            gi = band_in[m, 3].astype(jnp.float32) * on
            return (acc[0] + (lr * gr + li * gi), acc[1] + (li * gr - lr * gi))

        acc = (jnp.zeros((rows, n), jnp.float32), jnp.zeros((rows, n), jnp.float32))
        if peers <= 16:
            for e in range(peers):
                acc = term(e, acc)
        else:
            acc = lax.fori_loop(0, peers, term, acc)
        return energy_step * acc[0], energy_step * acc[1]

    def owned(j, carry):
        owner = lax.rem(me + j, peers)
        for i in range(kept):
            re, im = frequency(owner, i)
            pol_out[owner, i, 0] = re
            pol_out[owner, i, 1] = im

        pol_copy(j).start()
        return carry

    lax.fori_loop(1, peers, owned, 0)
    for i in range(kept):
        re, im = frequency(me, i)
        pol_in[me, i, 0] = re
        pol_in[me, i, 1] = im
    each(pol_copy, lambda c: c.wait_recv())
    for e in range(peers):
        for i in range(kept):
            for c in range(2):
                out_ref[c, i, 0, e * rows : (e + 1) * rows, :] = pol_in[e, i, c]

    each(band_copy, lambda c: c.wait_send())
    each(pol_copy, lambda c: c.wait_send())

    @pl.when(gives)
    def _():
        link(0, u, u_in, pos + 1).wait_send()

    @pl.when(jnp.logical_not(is_end))
    def _():
        link(3, full, g_in, outer).wait_send()


def local(onsite, coupling, damping, occupation, block_sizes, offsets):
    n = onsite.shape[-1]
    regions = lax.axis_size("region")
    peers = lax.axis_size("energy")
    rows = BAND // peers
    kept = offsets.shape[0] // peers
    block = pltpu.VMEM((n, 2 * n), jnp.float32)
    return pl.pallas_call(
        functools.partial(kernel, regions, peers),
        in_specs=[SM, SM, SM, VM, VM, VM],
        out_specs=VM,
        out_shape=jax.ShapeDtypeStruct((2, kept, 1, BAND, n), jnp.float32),
        scratch_shapes=[block] * 11
        + [
            pltpu.VMEM((2 * n, 2 * n), jnp.float32),
            pltpu.VMEM((peers, 4, rows, n), jnp.bfloat16),
            pltpu.VMEM((peers, 4, rows, n), jnp.bfloat16),
            pltpu.VMEM((peers, kept, 2, rows, n), jnp.float32),
            pltpu.VMEM((peers, kept, 2, rows, n), jnp.float32),
            pltpu.SemaphoreType.DMA((4,)),
            pltpu.SemaphoreType.DMA((4,)),
        ]
        + [pltpu.SemaphoreType.DMA((peers,))] * 4,
        compiler_params=pltpu.CompilerParams(collective_id=0, has_side_effects=True),
    )(block_sizes, occupation, offsets, onsite, coupling, damping)


def solution(mesh):
    placed = (
        P("region", None, None, None),
        P("region", None, None, None),
        P("region", None),
        P("energy", "region"),
        P("region"),
        P(),
    )
    return jax.shard_map(
        local,
        mesh=mesh,
        in_specs=placed,
        out_specs=P(None, "energy", "region", None, None),
        check_vma=False,
    )
```

```python
import functools
import jax
import jax.numpy as jnp
from jax import lax
from jax.experimental import pallas as pl
from jax.experimental.pallas import tpu as pltpu
from jax.sharding import PartitionSpec as P

BAND = 96
PANEL = 8

energy_step = 0.1
left_lead = 0.5

VM = pl.BlockSpec(memory_space=pltpu.VMEM)
SM = pl.BlockSpec(memory_space=pltpu.SMEM)


def dot(x, y):
    return jnp.dot(x, y, precision=lax.Precision.HIGHEST, preferred_element_type=jnp.float32)


def halves(x):
    n = x.shape[-1] // 2
    return x[:, :n], x[:, n:]


def cat(re, im):
    return jnp.concatenate([re, im], axis=1)


def adjoint(x):
    re, im = halves(x)
    return cat(re.T, -im.T)


def cmul(x, y):
    re, im = halves(y)
    return dot(x, jnp.concatenate([y, cat(-im, re)], axis=0))


def lane_bcast(x, j):
    return jnp.broadcast_to(x[:, j : j + 1], x.shape)


def row_bcast(x, k):
    return jnp.broadcast_to(x[k : k + 1, :], x.shape)


def lookahead(x, cols, z):
    terms = []
    for j, (cr, ci) in enumerate(cols):
        rr, ri = row_bcast(z[0], j), row_bcast(z[1], j)
        terms.append((cr * rr - ci * ri, cr * ri + ci * rr))
    while len(terms) > 1:
        terms = [(p[0] + q[0], p[1] + q[1]) for p, q in zip(terms[::2], terms[1::2])]
    return x[0] - terms[0][0], x[1] - terms[0][1]


def turned(x, start):
    n = x[0].shape[1]
    turn = (2 * n - start) % n
    return pltpu.roll(x[0], turn, 1), pltpu.roll(x[1], turn, 1)


def factor(x, front, start):
    n = x[0].shape[1]
    lane = lax.broadcasted_iota(jnp.int32, (PANEL, n), 1)
    sub = lax.broadcasted_iota(jnp.int32, (PANEL, n), 0)
    cols = [(lane_bcast(front[0], j), lane_bcast(front[1], j)) for j in range(PANEL)]
    ahead = turned(x, start + PANEL)
    for (re, im), at in ((x, lane - start), (ahead, lane - (n - PANEL))):
        inside = (at >= 0) & (at < PANEL)
        cols.append(
            (jnp.where(inside, (at == sub).astype(jnp.float32), re), jnp.where(inside, 0.0, im))
        )
    for k in range(PANEL):
        br, bi = cols[k]
        pr, pi = row_bcast(br, k), row_bcast(bi, k)
        scale = 1.0 / (pr * pr + pi * pi)
        here = sub == k
        qr = jnp.where(here, -pr, br * pr + bi * pi)
        qi = jnp.where(here, pi, bi * pr - br * pi)
        mr, mi = qr * scale, qi * scale
        for j in range(k + 1, len(cols)):
            cr, ci = cols[j]
            rr, ri = row_bcast(cr, k), row_bcast(ci, k)
            cols[j] = (
                jnp.where(here, 0.0, cr) - (mr * rr - mi * ri),
                jnp.where(here, 0.0, ci) - (mr * ri + mi * rr),
            )
    return cols[PANEL], cols[PANEL + 1]


def invert(a, rhs):
    n = a.shape[0]
    rhs[...] = jnp.zeros_like(rhs)
    lane = lax.broadcasted_iota(jnp.int32, (PANEL, n), 1)
    wide = lax.broadcasted_iota(jnp.int32, (n, 2 * n), 1) % n
    zero = jnp.zeros((PANEL, 2 * n), jnp.float32)

    def places(start):
        return pl.ds(start, PANEL), pl.ds(pl.multiple_of(n + start, PANEL), PANEL)

    def put(start, z):
        rows, low = places(start)
        rhs[rows, :] = cat(z[0], z[1])
        rhs[low, :] = cat(-z[1], z[0])

    def updated(start):
        old = a[...]
        keep = (wide < start) | (wide >= start + PANEL)
        return jnp.where(keep, old, 0.0) - dot(old, rhs[...])

    def columns(x, start):
        side = turned(x, start)
        return tuple((lane_bcast(side[0], j), lane_bcast(side[1], j)) for j in range(PANEL))

    def without(x, start):
        there = (lane >= start) & (lane < start + PANEL)
        return tuple(jnp.where(there, 0.0, v) for v in x)

    def following(start):
        begin = pl.multiple_of(jnp.minimum(start + PANEL, n - PANEL), PANEL)
        return halves(a[pl.ds(begin, PANEL), :])

    def prepare(x, start):
        front = tuple(jnp.where(lane >= n - PANEL, 0.0, v) for v in turned(x, start + PANEL))
        return without(x, start), front, columns(x, start)

    x = halves(a[:PANEL, :])
    first = factor(x, x, 0)
    put(0, first[0])

    def block(b, carry):
        (z, ahead), (x, front, cols) = carry
        last = pl.multiple_of((b - 1) * PANEL, PANEL)
        start = pl.multiple_of(b * PANEL, PANEL)
        later = following(start)
        later = lookahead(without(later, last), columns(later, last), z)
        later = prepare(later, start)
        new = updated(last)
        x = lookahead(x, cols, z)
        front = lookahead(front, cols, ahead)
        fresh = factor(x, front, start)
        a[...] = new
        a[pl.ds(last, PANEL), :] = cat(z[0], z[1])
        rows, low = places(last)
        rhs[rows, :] = zero
        rhs[low, :] = zero
        put(start, fresh[0])
        return fresh, later

    (z, _), _ = lax.fori_loop(1, n // PANEL, block, (first, prepare(following(0), 0)))
    last = n - PANEL
    a[...] = updated(last)
    a[pl.ds(last, PANEL), :] = cat(z[0], z[1])


def build(regions, total, size, onsite, coupling, damping):
    n = onsite.shape[-1]
    row = lax.broadcasted_iota(jnp.int32, (n, n), 0)
    col = lax.broadcasted_iota(jnp.int32, (n, n), 1)
    mask = ((row < size) & (col < size)).astype(jnp.float32)
    eye = row == col
    region = lax.axis_index("region")
    energy = energy_step * (lax.axis_index("energy") - total // 2).astype(jnp.float32)
    o_re, o_im = onsite[0, 0], onsite[0, 1]
    h_re = 0.5 * (o_re + o_re.T) * mask
    h_im = 0.5 * (o_im - o_im.T) * mask
    u = cat(coupling[0, 0] * mask, coupling[0, 1] * mask)
    diag_im = jnp.broadcast_to(damping[...], (n, n)) + jnp.where(region == 0, left_lead, 0.0)
    a_re = jnp.where(eye, energy, 0.0) - h_re
    a_im = jnp.where(eye, diag_im, 0.0) - h_im
    return cat(a_re, a_im), u


def skew(t):
    n = t.shape[0]
    col = lax.broadcasted_iota(jnp.int32, (n, n), 1)
    bit = 1
    while bit < n:
        moved = jnp.concatenate([t[bit:], t[:bit]], axis=0)
        t = jnp.where((col // bit) % 2 == 1, moved, t)
        bit *= 2
    return t


def band_values(g, size, weight):
    re, im = halves(g)
    t_re = -(im + im.T)
    t_im = re.T - re
    n = re.shape[0]
    row = lax.broadcasted_iota(jnp.int32, (BAND, n), 0)
    col = lax.broadcasted_iota(jnp.int32, (BAND, n), 1)
    valid = (row + col < size).astype(jnp.float32)
    b_re = skew(t_re)[:BAND] * valid
    b_im = skew(t_im)[:BAND] * valid
    return [
        (weight * b_re),
        (weight * b_im),
        ((1.0 - weight) * b_re),
        ((1.0 - weight) * b_im),
    ]


def send(src, dst, sems, axis, index):
    return pltpu.make_async_remote_copy(
        src_ref=src,
        dst_ref=dst,
        send_sem=sems[0],
        recv_sem=sems[1],
        device_id={axis: index},
        device_id_type=pl.DeviceIdType.MESH,
    )


def kernel(
    regions, peers, sizes, occ, offsets, onsite, coupling, damping, out_ref,
    a, g, w, u, u_in, s_out, s_in, m_out, m_in, g_in, full, rhs,
    band_out, band_in, pol_out, pol_in,
    link_send, link_recv, band_send, band_recv, pol_send, pol_recv,
):
    half = regions // 2
    pos = lax.axis_index("region")
    me = lax.axis_index("energy")
    left = pos < half
    inner = jnp.where(left, pos + 1, pos - 1)
    outer = jnp.where(left, pos - 1, pos + 1)
    is_mid = (pos == half - 1) | (pos == half)
    is_end = (pos == 0) | (pos == regions - 1)

    barrier = pltpu.get_barrier_semaphore()

    def greet(axis, index):
        pl.semaphore_signal(
            barrier, inc=1, device_id={axis: index}, device_id_type=pl.DeviceIdType.MESH
        )

    greet("region", inner)

    @pl.when(jnp.logical_not(is_end))
    def _():
        greet("region", outer)

    def greet_peer(j, carry):
        greet("energy", lax.rem(me + j, peers))
        return carry

    lax.fori_loop(1, peers, greet_peer, 0)

    a0, u0 = build(regions, peers, sizes[0], onsite, coupling, damping)
    u[...] = u0
    w[...] = u0
    a[...] = a0

    gives = (pos >= half - 1) & (pos < regions - 1)
    early = jnp.logical_not(is_end) | gives

    def enter():
        pl.semaphore_wait(barrier, jnp.where(is_end, peers, peers + 1))

    pl.when(early)(enter)

    def link(i, src, dst, index):
        return send(src, dst, (link_send.at[i], link_recv.at[i]), "region", index)

    @pl.when(gives)
    def _():
        link(0, u, u_in, pos + 1).start()

    @pl.when(pos == regions - 1)
    def _():
        l_re, l_im = halves(cmul(u0, adjoint(u0)))
        a[...] = a0 + cat(-l_im, l_re)

    @pl.when(jnp.logical_not(is_end))
    def _():
        link(1, s_out, s_in, outer).wait_recv()

        @pl.when(left)
        def _():
            a[...] = a[...] - s_in[...]

        @pl.when(jnp.logical_not(left))
        def _():
            uv = u[...]
            a[...] = a[...] - cmul(cmul(uv, s_in[...]), adjoint(uv))

    g[...] = a[...]
    invert(g, rhs)
    pl.when(jnp.logical_not(early))(enter)

    own = link(1, s_out, s_in, inner)

    @pl.when(jnp.logical_not(left))
    def _():
        @pl.when(jnp.logical_not(is_mid))
        def _():
            s_out[...] = g[...]
            own.start()

        link(0, u, u_in, pos - 1).wait_recv()
        w[...] = adjoint(u_in[...])

    @pl.when(is_mid)
    def _():
        wv = w[...]
        m_out[...] = cmul(cmul(adjoint(wv), g[...]), wv)
        copy = link(2, m_out, m_in, inner)
        copy.start()
        copy.wait_recv()
        full[...] = a[...] - m_in[...]
        invert(full, rhs)
        copy.wait_send()

    @pl.when(jnp.logical_not(is_mid))
    def _():
        wv = w[...]
        wg = cmul(adjoint(wv), g[...])

        @pl.when(left)
        def _():
            s_out[...] = cmul(wg, wv)
            own.start()

        gw = cmul(g[...], wv)
        link(3, full, g_in, inner).wait_recv()
        full[...] = g[...] + cmul(cmul(gw, g_in[...]), wg)
        own.wait_send()

    @pl.when(jnp.logical_not(is_end))
    def _():
        link(3, full, g_in, outer).start()

    rows = BAND // peers
    n = onsite.shape[-1]
    for c, v in enumerate(band_values(full[...], sizes[0], occ[0, 0])):
        v = v.astype(jnp.bfloat16)
        for e in range(peers):
            band_out[e, c] = v[e * rows : (e + 1) * rows]

    def band_copy(j):
        peer = lax.rem(me + j, peers)
        return send(
            band_out.at[peer], band_in.at[me], (band_send.at[j], band_recv.at[j]), "energy", peer
        )

    def each(make, act):
        def one(j, carry):
            act(make(j))
            return carry

        lax.fori_loop(1, peers, one, 0)

    each(band_copy, lambda c: c.start())
    band_in[me] = band_out[me]
    each(band_copy, lambda c: c.wait_recv())

    kept = offsets.shape[0] // peers

    def pol_copy(j):
        peer = lax.rem(me + j, peers)
        return send(
            pol_out.at[peer], pol_in.at[me], (pol_send.at[j], pol_recv.at[j]), "energy", peer
        )

    def frequency(owner, i):
        offset = offsets[owner * kept + i]

        def term(e, acc):
            m = e - offset
            on = jnp.where((m >= 0) & (m < peers), 1.0, 0.0)
            m = jnp.clip(m, 0, peers - 1)
            lr = band_in[e, 0].astype(jnp.float32)
            li = band_in[e, 1].astype(jnp.float32)
            gr = band_in[m, 2].astype(jnp.float32) * on
            gi = band_in[m, 3].astype(jnp.float32) * on
            return (acc[0] + (lr * gr + li * gi), acc[1] + (li * gr - lr * gi))

        acc = (jnp.zeros((rows, n), jnp.float32), jnp.zeros((rows, n), jnp.float32))
        if peers <= 16:
            for e in range(peers):
                acc = term(e, acc)
        else:
            acc = lax.fori_loop(0, peers, term, acc)
        return energy_step * acc[0], energy_step * acc[1]

    def owned(j, carry):
        owner = lax.rem(me + j, peers)
        for i in range(kept):
            re, im = frequency(owner, i)
            pol_out[owner, i, 0] = re
            pol_out[owner, i, 1] = im

        pol_copy(j).start()
        return carry

    lax.fori_loop(1, peers, owned, 0)
    for i in range(kept):
        re, im = frequency(me, i)
        pol_in[me, i, 0] = re
        pol_in[me, i, 1] = im
    each(pol_copy, lambda c: c.wait_recv())
    for e in range(peers):
        for i in range(kept):
            for c in range(2):
                out_ref[c, i, 0, e * rows : (e + 1) * rows, :] = pol_in[e, i, c]

    each(band_copy, lambda c: c.wait_send())
    each(pol_copy, lambda c: c.wait_send())

    @pl.when(gives)
    def _():
        link(0, u, u_in, pos + 1).wait_send()

    @pl.when(jnp.logical_not(is_end))
    def _():
        link(3, full, g_in, outer).wait_send()


def local(onsite, coupling, damping, occupation, block_sizes, offsets):
    n = onsite.shape[-1]
    regions = lax.axis_size("region")
    peers = lax.axis_size("energy")
    rows = BAND // peers
    kept = offsets.shape[0] // peers
    block = pltpu.VMEM((n, 2 * n), jnp.float32)
    return pl.pallas_call(
        functools.partial(kernel, regions, peers),
        in_specs=[SM, SM, SM, VM, VM, VM],
        out_specs=VM,
        out_shape=jax.ShapeDtypeStruct((2, kept, 1, BAND, n), jnp.float32),
        scratch_shapes=[block] * 11
        + [
            pltpu.VMEM((2 * n, 2 * n), jnp.float32),
            pltpu.VMEM((peers, 4, rows, n), jnp.bfloat16),
            pltpu.VMEM((peers, 4, rows, n), jnp.bfloat16),
            pltpu.VMEM((peers, kept, 2, rows, n), jnp.float32),
            pltpu.VMEM((peers, kept, 2, rows, n), jnp.float32),
            pltpu.SemaphoreType.DMA((4,)),
            pltpu.SemaphoreType.DMA((4,)),
        ]
        + [pltpu.SemaphoreType.DMA((peers,))] * 4,
        compiler_params=pltpu.CompilerParams(collective_id=0, has_side_effects=True),
    )(block_sizes, occupation, offsets, onsite, coupling, damping)


def solution(mesh):
    placed = (
        P("region", None, None, None),
        P("region", None, None, None),
        P("region", None),
        P("energy", "region"),
        P("region"),
        P(),
    )
    return jax.shard_map(
        local,
        mesh=mesh,
        in_specs=placed,
        out_specs=P(None, "energy", "region", None, None),
        check_vma=False,
    )
```

```python
import functools
import jax
import jax.numpy as jnp
from jax import lax
from jax.experimental import pallas as pl
from jax.experimental.pallas import tpu as pltpu
from jax.sharding import PartitionSpec as P

BAND = 96
PANEL = 8

energy_step = 0.1
left_lead = 0.5

VM = pl.BlockSpec(memory_space=pltpu.VMEM)
SM = pl.BlockSpec(memory_space=pltpu.SMEM)


def dot(x, y):
    return jnp.dot(x, y, precision=lax.Precision.HIGHEST, preferred_element_type=jnp.float32)


def halves(x):
    n = x.shape[-1] // 2
    return x[:, :n], x[:, n:]


def cat(re, im):
    return jnp.concatenate([re, im], axis=1)


def adjoint(x):
    re, im = halves(x)
    return cat(re.T, -im.T)


def cmul(x, y):
    re, im = halves(y)
    return dot(x, jnp.concatenate([y, cat(-im, re)], axis=0))


def lane_bcast(x, j):
    return jnp.broadcast_to(x[:, j : j + 1], x.shape)


def row_bcast(x, k):
    return jnp.broadcast_to(x[k : k + 1, :], x.shape)


def lookahead(x, cols, z):
    terms = []
    for j, (cr, ci) in enumerate(cols):
        rr, ri = row_bcast(z[0], j), row_bcast(z[1], j)
        terms.append((cr * rr - ci * ri, cr * ri + ci * rr))
    while len(terms) > 1:
        terms = [(p[0] + q[0], p[1] + q[1]) for p, q in zip(terms[::2], terms[1::2])]
    return x[0] - terms[0][0], x[1] - terms[0][1]


def turned(x, start):
    n = x[0].shape[1]
    turn = (2 * n - start) % n
    return pltpu.roll(x[0], turn, 1), pltpu.roll(x[1], turn, 1)


def factor(x, front, start):
    n = x[0].shape[1]
    lane = lax.broadcasted_iota(jnp.int32, (PANEL, n), 1)
    sub = lax.broadcasted_iota(jnp.int32, (PANEL, n), 0)
    cols = [(lane_bcast(front[0], j), lane_bcast(front[1], j)) for j in range(PANEL)]
    ahead = turned(x, start + PANEL)
    for (re, im), at in ((x, lane - start), (ahead, lane - (n - PANEL))):
        inside = (at >= 0) & (at < PANEL)
        cols.append(
            (jnp.where(inside, (at == sub).astype(jnp.float32), re), jnp.where(inside, 0.0, im))
        )
    for k in range(PANEL):
        br, bi = cols[k]
        pr, pi = row_bcast(br, k), row_bcast(bi, k)
        scale = 1.0 / (pr * pr + pi * pi)
        here = sub == k
        qr = jnp.where(here, -pr, br * pr + bi * pi)
        qi = jnp.where(here, pi, bi * pr - br * pi)
        mr, mi = qr * scale, qi * scale
        for j in range(k + 1, len(cols)):
            cr, ci = cols[j]
            rr, ri = row_bcast(cr, k), row_bcast(ci, k)
            cols[j] = (
                jnp.where(here, 0.0, cr) - (mr * rr - mi * ri),
                jnp.where(here, 0.0, ci) - (mr * ri + mi * rr),
            )
    return cols[PANEL], cols[PANEL + 1]


def invert(a, rhs):
    n = a.shape[0]
    rhs[...] = jnp.zeros_like(rhs)
    lane = lax.broadcasted_iota(jnp.int32, (PANEL, n), 1)
    wide = lax.broadcasted_iota(jnp.int32, (n, 2 * n), 1) % n
    zero = jnp.zeros((PANEL, 2 * n), jnp.float32)

    def places(start):
        return pl.ds(start, PANEL), pl.ds(pl.multiple_of(n + start, PANEL), PANEL)

    def put(start, z):
        rows, low = places(start)
        rhs[rows, :] = cat(z[0], z[1])
        rhs[low, :] = cat(-z[1], z[0])

    def updated(start):
        old = a[...]
        keep = (wide < start) | (wide >= start + PANEL)
        return jnp.where(keep, old, 0.0) - dot(old, rhs[...])

    def columns(x, start):
        side = turned(x, start)
        return tuple((lane_bcast(side[0], j), lane_bcast(side[1], j)) for j in range(PANEL))

    def without(x, start):
        there = (lane >= start) & (lane < start + PANEL)
        return tuple(jnp.where(there, 0.0, v) for v in x)

    def following(start):
        begin = pl.multiple_of(jnp.minimum(start + PANEL, n - PANEL), PANEL)
        return halves(a[pl.ds(begin, PANEL), :])

    def prepare(x, start):
        front = tuple(jnp.where(lane >= n - PANEL, 0.0, v) for v in turned(x, start + PANEL))
        return without(x, start), front, columns(x, start)

    x = halves(a[:PANEL, :])
    first = factor(x, x, 0)
    put(0, first[0])

    def block(b, carry):
        (z, ahead), (x, front, cols) = carry
        last = pl.multiple_of((b - 1) * PANEL, PANEL)
        start = pl.multiple_of(b * PANEL, PANEL)
        later = following(start)
        later = lookahead(without(later, last), columns(later, last), z)
        later = prepare(later, start)
        new = updated(last)
        x = lookahead(x, cols, z)
        front = lookahead(front, cols, ahead)
        fresh = factor(x, front, start)
        a[...] = new
        a[pl.ds(last, PANEL), :] = cat(z[0], z[1])
        rows, low = places(last)
        rhs[rows, :] = zero
        rhs[low, :] = zero
        put(start, fresh[0])
        return fresh, later

    (z, _), _ = lax.fori_loop(1, n // PANEL, block, (first, prepare(following(0), 0)))
    last = n - PANEL
    a[...] = updated(last)
    a[pl.ds(last, PANEL), :] = cat(z[0], z[1])


def build(regions, total, size, onsite, coupling, damping):
    n = onsite.shape[-1]
    row = lax.broadcasted_iota(jnp.int32, (n, n), 0)
    col = lax.broadcasted_iota(jnp.int32, (n, n), 1)
    mask = ((row < size) & (col < size)).astype(jnp.float32)
    eye = row == col
    region = lax.axis_index("region")
    energy = energy_step * (lax.axis_index("energy") - total // 2).astype(jnp.float32)
    o_re, o_im = onsite[0, 0], onsite[0, 1]
    h_re = 0.5 * (o_re + o_re.T) * mask
    h_im = 0.5 * (o_im - o_im.T) * mask
    u = cat(coupling[0, 0] * mask, coupling[0, 1] * mask)
    diag_im = jnp.broadcast_to(damping[...], (n, n)) + jnp.where(region == 0, left_lead, 0.0)
    a_re = jnp.where(eye, energy, 0.0) - h_re
    a_im = jnp.where(eye, diag_im, 0.0) - h_im
    return cat(a_re, a_im), u


def skew(t):
    n = t.shape[0]
    col = lax.broadcasted_iota(jnp.int32, (n, n), 1)
    bit = 1
    while bit < n:
        moved = jnp.concatenate([t[bit:], t[:bit]], axis=0)
        t = jnp.where((col // bit) % 2 == 1, moved, t)
        bit *= 2
    return t


def band_values(g, size, weight):
    re, im = halves(g)
    t_re = -(im + im.T)
    t_im = re.T - re
    n = re.shape[0]
    row = lax.broadcasted_iota(jnp.int32, (BAND, n), 0)
    col = lax.broadcasted_iota(jnp.int32, (BAND, n), 1)
    valid = (row + col < size).astype(jnp.float32)
    b_re = skew(t_re)[:BAND] * valid
    b_im = skew(t_im)[:BAND] * valid
    return [
        (weight * b_re),
        (weight * b_im),
        ((1.0 - weight) * b_re),
        ((1.0 - weight) * b_im),
    ]


def send(src, dst, sems, axis, index):
    return pltpu.make_async_remote_copy(
        src_ref=src,
        dst_ref=dst,
        send_sem=sems[0],
        recv_sem=sems[1],
        device_id={axis: index},
        device_id_type=pl.DeviceIdType.MESH,
    )


def kernel(
    regions, peers, sizes, occ, offsets, onsite, coupling, damping, out_ref,
    a, g, w, wh, u, uh, u_in, s_out, s_in, m_out, m_in, g_in, full, rhs,
    band_out, band_in, pol_out, pol_in,
    link_send, link_recv, band_send, band_recv, pol_send, pol_recv,
):
    half = regions // 2
    pos = lax.axis_index("region")
    me = lax.axis_index("energy")
    left = pos < half
    inner = jnp.where(left, pos + 1, pos - 1)
    outer = jnp.where(left, pos - 1, pos + 1)
    is_mid = (pos == half - 1) | (pos == half)
    is_end = (pos == 0) | (pos == regions - 1)

    barrier = pltpu.get_barrier_semaphore()

    def greet(axis, index):
        pl.semaphore_signal(
            barrier, inc=1, device_id={axis: index}, device_id_type=pl.DeviceIdType.MESH
        )

    greet("region", inner)

    @pl.when(jnp.logical_not(is_end))
    def _():
        greet("region", outer)

    def greet_peer(j, carry):
        greet("energy", lax.rem(me + j, peers))
        return carry

    lax.fori_loop(1, peers, greet_peer, 0)

    a0, u0 = build(regions, peers, sizes[0], onsite, coupling, damping)
    u0h = adjoint(u0)
    u[...] = u0
    uh[...] = u0h
    a[...] = a0

    gives = (pos >= half - 1) & (pos < regions - 1)
    early = jnp.logical_not(is_end) | gives

    def enter():
        pl.semaphore_wait(barrier, jnp.where(is_end, peers, peers + 1))

    pl.when(early)(enter)

    def link(i, src, dst, index):
        return send(src, dst, (link_send.at[i], link_recv.at[i]), "region", index)

    @pl.when(gives)
    def _():
        link(0, u, u_in, pos + 1).start()

    @pl.when(pos == regions - 1)
    def _():
        l_re, l_im = halves(cmul(u0, u0h))
        a[...] = a0 + cat(-l_im, l_re)

    def below():
        link(0, u, u_in, pos - 1).wait_recv()
        w[...] = adjoint(u_in[...])
        wh[...] = u_in[...]

    @pl.when(left)
    def _():
        w[...] = u0
        wh[...] = u0h

    @pl.when(jnp.logical_not(left) & jnp.logical_not(is_end))
    def _():
        below()

    @pl.when(jnp.logical_not(is_end))
    def _():
        link(1, s_out, s_in, outer).wait_recv()

        @pl.when(left)
        def _():
            a[...] = a[...] - s_in[...]

        @pl.when(jnp.logical_not(left))
        def _():
            a[...] = a[...] - cmul(cmul(u[...], s_in[...]), uh[...])

    g[...] = a[...]
    invert(g, rhs)
    pl.when(jnp.logical_not(early))(enter)

    own = link(1, s_out, s_in, inner)

    @pl.when(jnp.logical_not(left))
    def _():
        @pl.when(jnp.logical_not(is_mid))
        def _():
            s_out[...] = g[...]
            own.start()

        pl.when(is_end)(below)

    @pl.when(is_mid)
    def _():
        m_out[...] = cmul(cmul(wh[...], g[...]), w[...])
        copy = link(2, m_out, m_in, inner)
        copy.start()
        copy.wait_recv()
        full[...] = a[...] - m_in[...]
        invert(full, rhs)
        copy.wait_send()

    @pl.when(jnp.logical_not(is_mid))
    def _():
        wv = w[...]
        wg = cmul(wh[...], g[...])

        @pl.when(left)
        def _():
            s_out[...] = cmul(wg, wv)
            own.start()

        gw = cmul(g[...], wv)
        link(3, full, g_in, inner).wait_recv()
        full[...] = g[...] + cmul(cmul(gw, g_in[...]), wg)
        own.wait_send()

    @pl.when(jnp.logical_not(is_end))
    def _():
        link(3, full, g_in, outer).start()

    rows = BAND // peers
    n = onsite.shape[-1]
    for c, v in enumerate(band_values(full[...], sizes[0], occ[0, 0])):
        v = v.astype(jnp.bfloat16)
        for e in range(peers):
            band_out[e, c] = v[e * rows : (e + 1) * rows]

    def band_copy(j):
        peer = lax.rem(me + j, peers)
        return send(
            band_out.at[peer], band_in.at[me], (band_send.at[j], band_recv.at[j]), "energy", peer
        )

    def each(make, act):
        def one(j, carry):
            act(make(j))
            return carry

        lax.fori_loop(1, peers, one, 0)

    each(band_copy, lambda c: c.start())
    band_in[me] = band_out[me]
    each(band_copy, lambda c: c.wait_recv())

    kept = offsets.shape[0] // peers

    def pol_copy(j):
        peer = lax.rem(me + j, peers)
        return send(
            pol_out.at[peer], pol_in.at[me], (pol_send.at[j], pol_recv.at[j]), "energy", peer
        )

    def frequency(owner, i):
        offset = offsets[owner * kept + i]

        def term(e, acc):
            m = e - offset
            on = jnp.where((m >= 0) & (m < peers), 1.0, 0.0)
            m = jnp.clip(m, 0, peers - 1)
            lr = band_in[e, 0].astype(jnp.float32)
            li = band_in[e, 1].astype(jnp.float32)
            gr = band_in[m, 2].astype(jnp.float32) * on
            gi = band_in[m, 3].astype(jnp.float32) * on
            return (acc[0] + (lr * gr + li * gi), acc[1] + (li * gr - lr * gi))

        acc = (jnp.zeros((rows, n), jnp.float32), jnp.zeros((rows, n), jnp.float32))
        if peers <= 16:
            for e in range(peers):
                acc = term(e, acc)
        else:
            acc = lax.fori_loop(0, peers, term, acc)
        return energy_step * acc[0], energy_step * acc[1]

    def owner_values(owner):
        return jnp.concatenate([v for i in range(kept) for v in frequency(owner, i)], axis=0)

    def owned(j, carry):
        owner = lax.rem(me + j, peers)
        pol_out[owner] = owner_values(owner)
        pol_copy(j).start()
        return carry

    lax.fori_loop(1, peers, owned, 0)
    pol_in[me] = owner_values(me)
    each(pol_copy, lambda c: c.wait_recv())
    for e in range(peers):
        for i in range(kept):
            for c in range(2):
                begin = (2 * i + c) * rows
                out_ref[c, i, 0, e * rows : (e + 1) * rows, :] = pol_in[e, begin : begin + rows]

    each(band_copy, lambda c: c.wait_send())
    each(pol_copy, lambda c: c.wait_send())

    @pl.when(gives)
    def _():
        link(0, u, u_in, pos + 1).wait_send()

    @pl.when(jnp.logical_not(is_end))
    def _():
        link(3, full, g_in, outer).wait_send()


def local(onsite, coupling, damping, occupation, block_sizes, offsets):
    n = onsite.shape[-1]
    regions = lax.axis_size("region")
    peers = lax.axis_size("energy")
    rows = BAND // peers
    kept = offsets.shape[0] // peers
    block = pltpu.VMEM((n, 2 * n), jnp.float32)
    return pl.pallas_call(
        functools.partial(kernel, regions, peers),
        in_specs=[SM, SM, SM, VM, VM, VM],
        out_specs=VM,
        out_shape=jax.ShapeDtypeStruct((2, kept, 1, BAND, n), jnp.float32),
        scratch_shapes=[block] * 13
        + [
            pltpu.VMEM((2 * n, 2 * n), jnp.float32),
            pltpu.VMEM((peers, 4, rows, n), jnp.bfloat16),
            pltpu.VMEM((peers, 4, rows, n), jnp.bfloat16),
            pltpu.VMEM((peers, 2 * kept * rows, n), jnp.float32),
            pltpu.VMEM((peers, 2 * kept * rows, n), jnp.float32),
            pltpu.SemaphoreType.DMA((4,)),
            pltpu.SemaphoreType.DMA((4,)),
        ]
        + [pltpu.SemaphoreType.DMA((peers,))] * 4,
        compiler_params=pltpu.CompilerParams(collective_id=0, has_side_effects=True),
    )(block_sizes, occupation, offsets, onsite, coupling, damping)


def solution(mesh):
    placed = (
        P("region", None, None, None),
        P("region", None, None, None),
        P("region", None),
        P("energy", "region"),
        P("region"),
        P(),
    )
    return jax.shard_map(
        local,
        mesh=mesh,
        in_specs=placed,
        out_specs=P(None, "energy", "region", None, None),
        check_vma=False,
    )
```
